256 devices in a mesh: tx: 4 (over y), ty: 2 (over z_lo), ea: 32 (over z_hi, x, core).
Axes of the slice: x: 4, y: 4, z: 8 (z_hi: 4, z_lo: 2; z = z_hi * 2 + z_lo), core: 2. Of those that a mesh axis runs over, the one named last changes fastest.
Arguments:
- science: float32 [32, 512, 512], P('ea', 'tx', 'ty'), may hold values from -6 to 6
- inv_variance: float32 [32, 512, 512], P('ea', 'tx', 'ty'), may hold values from 0.25 to 4
- psf_taps: float32 [32, 9], P('ea'), may hold values from 0.05 to 1
- epoch_times: int32 [32], replicated, may hold values from 0 to 256, as said below
- velocities: int32 [192, 2], P('ea'), may hold values from -15 to 15
Outputs:
- likelihood: float32 [192, 512, 512], P('ea', 'tx', 'ty')
The draws below stay inside these ranges and needn't reach their ends.
Inputs may be any that keep to these rules, and one draw needn't show every extreme that they name: `epoch_times`: the first epoch has time 0 and the last has time 256.
All inputs are finite; a program needn't handle non-finite values.
Results may differ from the reference program's by a relative error of at most 0.0053.
Values may be sent and summed in bfloat16 or wider, within the bound.
A program may use at most 64 MiB of HBM per device.

```python
import math
import jax
import jax.numpy as jnp
from jax import lax

REACH = 32
PR = 4
VMAX = 15
EPOCHS = 32
HYPS = 192
NROWS = 512
NCOLS = 512
TSPAN = 256
TAPS = 9


def draw_epoch_times(key, part):
    values = jax.random.randint(key, (EPOCHS,), 0, TSPAN + 1).astype(jnp.int32)
    values = values.at[0].set(0)
    values = values.at[EPOCHS - 1].set(TSPAN)
    return values


def plant(result, own_key, low, top_value):
    longest = result.shape.index(max(result.shape))
    spots = []
    for shift in (0, 1):
        where = [jax.random.randint(jax.random.fold_in(own_key, axis), (), 0, length) for axis, length in enumerate(result.shape)]
        where[longest] = (where[longest] + shift) % result.shape[longest]
        spots.append(tuple(where))
    return result.at[spots[0]].set(low).at[spots[1]].set(top_value)


def block_scale(key, shape, shards, low, largest):
    factor_of = 1.0
    for axis_at, parts in shards:
        draws = jax.random.uniform(jax.random.fold_in(jax.random.fold_in(key, 6), axis_at), (parts,), jnp.float32, low / len(shards), largest / len(shards))
        factor_of = factor_of * jnp.repeat(jnp.exp(draws), shape[axis_at] // parts).reshape((-1,) + (1,) * (len(shape) - 1 - axis_at))
    return factor_of


def normal_values(rng, extent, spread, most, shards=(), kind=jnp.bfloat16):
    result = spread * jax.random.normal(rng, extent, jnp.float32)
    if shards:
        result = result * block_scale(rng, extent, shards, -0.22, 0.18)
    return jnp.clip(result, -most, most).astype(kind)


def setup_inputs(seed: int = 0) -> dict:
    seeds = jax.random.split(jax.random.key(seed), 6)
    return {
        "science": normal_values(seeds[0], (EPOCHS, NROWS, NCOLS), 1.0, 6.0, ((0, 32), (1, 4), (2, 2)), jnp.float32),
        "inv_variance": jnp.clip(jnp.exp(math.log(4.0) - 2.7725887 * jax.random.uniform(seeds[1], (EPOCHS, NROWS, NCOLS), jnp.float32) ** block_scale(seeds[1], (EPOCHS, NROWS, NCOLS), ((0, 32), (1, 4), (2, 2)), -0.2, 0.2)), 0.25, 4.0),
        "psf_taps": jnp.clip(jnp.exp(math.log(1.0) - 2.9957323 * jax.random.uniform(seeds[2], (EPOCHS, TAPS), jnp.float32) ** block_scale(seeds[2], (EPOCHS, TAPS), ((0, 32),), -0.2, 0.2)), 0.05, 1.0),
        "epoch_times": draw_epoch_times(jax.random.fold_in(seeds[5], 71), 0),
        "velocities": plant(jax.random.randint(seeds[4], (HYPS, 2), 0 - VMAX, VMAX + 1), jax.random.fold_in(seeds[4], 1), 0 - VMAX, VMAX).astype(jnp.int32),
    }


def blur(field, kern):
    count = kern.shape[1]
    rows = field.shape[1] - count + 1
    acc = kern[:, 0, None, None] * field[:, 0:rows, :]
    for k in range(1, count):
        acc = acc + kern[:, k, None, None] * field[:, k:k + rows, :]
    cols = acc.shape[2] - count + 1
    out = kern[:, 0, None, None] * acc[:, :, 0:cols]
    for k in range(1, count):
        out = out + kern[:, k, None, None] * acc[:, :, k:k + cols]
    return out

def spline_taps(speed, tvals):
    moved = jnp.floor_divide(speed * tvals, 8)
    whole = jnp.floor_divide(moved, 16)
    frac = (moved - 16 * whole).astype(jnp.float32) / 16.0
    frac2 = frac * frac
    frac3 = frac2 * frac
    weights = jnp.stack([(1.0 - frac) ** 3 / 6.0, (3.0 * frac3 - 6.0 * frac2 + 4.0) / 6.0, (-3.0 * frac3 + 3.0 * frac2 + 3.0 * frac + 1.0) / 6.0, frac3 / 6.0], -1)
    return (whole.astype(jnp.int32), weights.astype(jnp.bfloat16))

def reference(science, inv_variance, psf_taps, epoch_times, velocities):
    kern_p = psf_taps / lax.optimization_barrier(jnp.sum(psf_taps, axis=1, keepdims=True))
    kern_q = kern_p * kern_p
    weighted = science * inv_variance
    pad_psf = ((0, 0), (PR, PR), (PR, PR))
    psi = blur(jnp.pad(weighted, pad_psf), kern_p).astype(jnp.bfloat16)
    phi = blur(jnp.pad(inv_variance, pad_psf), kern_q).astype(jnp.bfloat16)
    images = jnp.stack([psi, phi], 1)
    padded = jnp.pad(images, ((0, 0), (0, 0), (REACH, REACH), (REACH, REACH)))

    def one_epoch(image, whole_r, w_r, whole_c, w_c):
        rows_acc = jnp.zeros((2, NROWS, padded.shape[3]), jnp.float32)
        for a in range(4):
            start = (REACH + whole_r + a - 1).astype(jnp.int32)
            piece = lax.dynamic_slice_in_dim(image, start, NROWS, axis=1).astype(jnp.float32)
            rows_acc = rows_acc + w_r[a].astype(jnp.float32) * piece
        moved_rows = rows_acc.astype(jnp.bfloat16)
        out = jnp.zeros((2, NROWS, NCOLS), jnp.float32)
        for b in range(4):
            start = (REACH + whole_c + b - 1).astype(jnp.int32)
            piece = lax.dynamic_slice_in_dim(moved_rows, start, NCOLS, axis=2).astype(jnp.float32)
            out = out + w_c[b].astype(jnp.float32) * piece
        return out

    def one_hyp(speed):
        whole_r, w_r = spline_taps(speed[0], epoch_times)
        whole_c, w_c = spline_taps(speed[1], epoch_times)
        terms = jax.vmap(one_epoch)(padded, whole_r, w_r, whole_c, w_c)
        sums = lax.optimization_barrier(jnp.sum(terms, axis=0))
        return sums[0] / jnp.sqrt(sums[1])
    return lax.map(one_hyp, velocities)
```

```python
import functools

import jax
import jax.numpy as jnp
import numpy as np
from jax import lax
from jax.experimental import pallas as pl
from jax.experimental.pallas import tpu as pltpu
from jax.sharding import PartitionSpec as P

MESH = pl.DeviceIdType.MESH
F32 = jnp.float32
BF16 = jnp.bfloat16
ROWS, COLS = 128, 256
HALO = 32
EDGE = 40
TAPS = 9
SPAN = COLS + HALO
EPOCHS = 32
GROUP = 8
FRACS = 16
HALF = SPAN // 2


def spline_table():
    frac = np.arange(FRACS, dtype=np.float32) / np.float32(16.0)
    frac2 = frac * frac
    frac3 = frac2 * frac
    one = np.float32(1.0)
    table = np.stack(
        [
            (one - frac) ** 3 / 6,
            (3 * frac3 - 6 * frac2 + 4) / 6,
            (-3 * frac3 + 3 * frac2 + 3 * frac + 1) / 6,
            frac3 / 6,
        ],
        -1,
    )
    return table.astype(np.float32).astype(BF16).astype(np.float32)


def shift_of(speed, time):
    moved = lax.shift_right_arithmetic(speed * time, 3)
    return lax.shift_right_arithmetic(moved, 4), lax.bitwise_and(moved, 15)


def band(offset, weights):
    out = jnp.zeros(offset.shape, F32)
    for a in range(4):
        out = jnp.where(offset == a, weights[a], out)
    return out


def build_templates(wtab, ty, col_main, col_rim, row_tmpl):
    k = lax.broadcasted_iota(jnp.int32, (320, 128), 1)
    u = lax.broadcasted_iota(jnp.int32, (320, 128), 0)
    main_offset = k - u + 33
    k2 = lax.broadcasted_iota(jnp.int32, (320, 128), 1) % 32 + jnp.where(ty == 0, COLS, -HALO)
    u2 = lax.broadcasted_iota(jnp.int32, (320, 128), 0)
    rim_offset = k2 - u2 + 33
    v = lax.broadcasted_iota(jnp.int32, (256, 128), 0)
    r = lax.broadcasted_iota(jnp.int32, (256, 128), 1)
    row_offset = v - 64 - r + 1

    @pl.loop(0, FRACS)
    def _(f):
        weights = [wtab[f, a] for a in range(4)]
        col_main[f, 0] = band(main_offset, weights)
        col_main[f, 1] = band(main_offset + 128, weights)
        col_rim[f] = band(rim_offset, weights)
        row_tmpl[f] = band(row_offset, weights)


def move_rows(epoch, place, times, vel, hyps, images, row_tmpl, rhs, moved):
    time = times[epoch]
    for h in range(hyps):
        whole, frac = shift_of(vel[h, 0], time)
        lanes = slice(h * ROWS, (h + 1) * ROWS)
        rhs[0:128, lanes] = row_tmpl[frac, pl.ds(64 - whole, 128), :].astype(BF16)
        rhs[128:160, lanes] = row_tmpl[frac, pl.ds(32 - whole, 32), :].astype(BF16)
        rhs[160:192, lanes] = row_tmpl[frac, pl.ds(192 - whole, 32), :].astype(BF16)
    rims = images[epoch, 2]
    swapped = jnp.concatenate([rims[:, 64:], rims[:, :64]], axis=1)
    left = (
        jnp.concatenate([images[epoch, 0], rims], axis=1),
        jnp.concatenate([images[epoch, 1], swapped], axis=1),
    )
    for pair in range(hyps // 2):
        right = rhs[:, pair * 256 : (pair + 1) * 256]
        for i in range(2):
            res = jnp.dot(left[i], right, preferred_element_type=F32).astype(BF16)
            for q in range(2):
                h = 2 * pair + q
                part = res[:, q * ROWS : (q + 1) * ROWS]
                main = pl.multiple_of(place * COLS, COLS)
                rim = pl.multiple_of(GROUP * COLS + place * HALO, HALO)
                moved[h, pl.ds(main, COLS), i * ROWS : (i + 1) * ROWS] = part[:COLS]
                moved[h, pl.ds(rim, HALO), i * ROWS : (i + 1) * ROWS] = part[COLS:]


def add_columns(h, first, times, vel, col_main, col_rim, bands, moved, acc):
    shifts = [shift_of(vel[h, 1], times[first + p]) for p in range(GROUP)]
    for p in range(GROUP):
        whole, frac = shifts[p]
        for q in range(2):
            lanes = slice(p * COLS + q * 128, p * COLS + (q + 1) * 128)
            bands[:, lanes] = col_main[frac, q, pl.ds(32 + whole, COLS), :].astype(BF16)
    group_of_lane = lax.broadcasted_iota(jnp.int32, (COLS, 128), 1) // 32
    for q in range(GROUP // 4):
        tile = None
        for p in range(4):
            whole, frac = shifts[4 * q + p]
            rows = col_rim[frac, pl.ds(32 + whole, COLS), :]
            tile = rows if tile is None else jnp.where(group_of_lane == p, rows, tile)
        bands[:, GROUP * COLS + q * 128 : GROUP * COLS + (q + 1) * 128] = tile.astype(BF16)
    acc[h] += jnp.dot(bands[...], moved[h], preferred_element_type=F32)


def kernel(
    hyps,
    times,
    vel,
    wtab,
    taps,
    science,
    inv_variance,
    out,
    images,
    raw,
    turned,
    col_main,
    col_rim,
    row_tmpl,
    rhs,
    moved,
    bands,
    acc,
    edge_send,
    edge_recv,
    send_sems,
    recv_sems,
):
    tx, ty, me = lax.axis_index("tx"), lax.axis_index("ty"), lax.axis_index("ea")
    core, x, z = lax.rem(me, 2), lax.rem(lax.div(me, 2), 4), lax.div(me, 8)

    def ident(dz, dx, other=False):
        c = 1 - core if other else core
        return lax.rem(z + dz, 4) * 8 + lax.rem(x + dx, 4) * 2 + c

    up, down = {"tx": lax.rem(tx + 3, 4)}, {"tx": lax.rem(tx + 1, 4)}
    beside = {"ty": 1 - ty}
    z_up, z_down = {"ea": ident(1, 0)}, {"ea": ident(3, 0)}
    x_up, x_down = {"ea": ident(0, 1)}, {"ea": ident(0, 3)}
    twin = {"ea": ident(0, 0, True)}

    barrier = pltpu.get_barrier_semaphore()
    for peer in (up, down, beside, z_up, z_down, x_up, x_down, twin):
        pl.semaphore_signal(barrier, inc=1, device_id=peer, device_id_type=MESH)

    ivar = inv_variance[0]
    raw[0, EDGE : EDGE + ROWS] = science[0] * ivar
    raw[1, EDGE : EDGE + ROWS] = ivar
    pl.semaphore_wait(barrier, 8)

    def edge_copy(src, dst, n, peer):
        return pltpu.make_async_remote_copy(
            src_ref=src, dst_ref=dst, send_sem=edge_send.at[n], recv_sem=edge_recv.at[n], device_id=peer, device_id_type=MESH
        )

    to_up = edge_copy(raw.at[:, EDGE : 2 * EDGE], raw.at[:, EDGE + ROWS : 2 * EDGE + ROWS], 0, up)
    to_down = edge_copy(raw.at[:, ROWS : ROWS + EDGE], raw.at[:, 0:EDGE], 1, down)
    to_up.start()
    to_down.start()

    build_templates(wtab, ty, col_main, col_rim, row_tmpl)
    rhs[192:256] = jnp.zeros((64, hyps * ROWS), BF16)
    acc[...] = jnp.zeros_like(acc)

    tap_p = taps[...] / jnp.sum(taps[...], axis=1, keepdims=True)
    tap_q = tap_p * tap_p

    def tap(which, t):
        return (tap_p, tap_q)[which][0:1, t : t + 1]

    to_up.wait()
    to_down.wait()
    for i in range(2):
        raw[i, 0:EDGE] = jnp.where(tx == 0, 0.0, raw[i, 0:EDGE])
        raw[i, EDGE + ROWS :] = jnp.where(tx == 3, 0.0, raw[i, EDGE + ROWS :])

    def row_blur(i, start, size):
        total = None
        for t in range(TAPS):
            term = tap(i, t) * raw[i, start + t - 4 : start + t - 4 + size]
            total = term if total is None else total + term
        return total

    far = jnp.where(ty == 0, 0, EDGE + COLS)
    near = jnp.where(ty == 0, EDGE + COLS, 0)
    rims = []
    for i in range(2):
        turned[i, EDGE : EDGE + COLS] = row_blur(i, EDGE, ROWS).T
        rims.append(jnp.where(tx == 0, 0.0, row_blur(i, EDGE - HALO, HALO)))
        rims.append(jnp.where(tx == 3, 0.0, row_blur(i, EDGE + ROWS, HALO)))
    turned[2, EDGE : EDGE + COLS] = jnp.concatenate(rims, axis=0).T
    turned[:, pl.ds(pl.multiple_of(far, 8), EDGE), :] = jnp.zeros((3, EDGE, 128), F32)
    to_beside = edge_copy(
        turned.at[:, pl.ds(pl.multiple_of(EDGE + jnp.where(ty == 0, COLS - EDGE, 0), 8), EDGE), :],
        turned.at[:, pl.ds(pl.multiple_of(far, 8), EDGE), :],
        2,
        beside,
    )
    to_beside.start()
    to_beside.wait()

    lane = lax.broadcasted_iota(jnp.int32, (1, 128), 1)

    def col_tap(b, t):
        if b < 2:
            return tap(b, t)
        return jnp.where(lane < 64, tap(0, t), tap(1, t))

    rim_start = jnp.where(ty == 0, EDGE + COLS, EDGE - HALO)
    for b in range(3):
        total, rim = None, None
        for t in range(TAPS):
            term = col_tap(b, t) * turned[b, EDGE + t - 4 : EDGE + t - 4 + COLS]
            total = term if total is None else total + term
            term = col_tap(b, t) * turned[b, pl.ds(rim_start + t - 4, HALO), :]
            rim = term if rim is None else rim + term
        images[me, b, 0:COLS] = total.astype(BF16)
        images[me, b, COLS:SPAN] = rim.astype(BF16)

    sends = []

    def view(block, part):
        if part is None:
            return images.at[block]
        return images.at[block, :, part * HALF : (part + 1) * HALF]

    def descriptor(block, part, peer, n):
        return pltpu.make_async_remote_copy(
            src_ref=view(block, part),
            dst_ref=view(block, part),
            send_sem=send_sems.at[n],
            recv_sem=recv_sems.at[block, 0 if part is None else part],
            device_id=peer,
            device_id_type=MESH,
        )

    def send(block, part, peer):
        copy = descriptor(block, part, peer, len(sends))
        copy.start()
        sends.append(copy)

    def arrived(block, part=None):
        descriptor(block, part, twin, 0).wait_recv()

    own = ident(0, 0)
    for peer in (z_up, z_down, x_up, x_down, twin):
        send(own, None, peer)

    def x_arrivals(dz):
        below, above, across = ident(dz, 3), ident(dz, 1), ident(dz, 2)
        arrived(below)
        send(below, 0, x_up)
        send(below, None, twin)
        arrived(above)
        send(above, 1, x_down)
        send(above, None, twin)
        return across

    def x_across(across):
        arrived(across, 0)
        arrived(across, 1)
        send(across, None, twin)

    def spread(block):
        send(block, None, x_up)
        send(block, None, x_down)
        send(block, None, twin)

    across0 = x_arrivals(0)
    low, high, opposite = ident(3, 0), ident(1, 0), ident(2, 0)
    arrived(low)
    send(low, 0, z_up)
    spread(low)
    arrived(high)
    send(high, 1, z_down)
    spread(high)
    x_across(across0)
    arrived(opposite, 0)
    arrived(opposite, 1)
    spread(opposite)
    acrosses = [x_arrivals(dz) for dz in (3, 1)]
    for across in acrosses:
        x_across(across)
    x_across(x_arrivals(2))
    for dz in range(4):
        for dx in range(4):
            arrived(ident(dz, dx, True))
    for copy in sends:
        copy.wait_send()

    @pl.loop(0, EPOCHS // GROUP)
    def _(g):
        first = g * GROUP

        @pl.loop(0, GROUP)
        def _(p):
            move_rows(first + p, p, times, vel, hyps, images, row_tmpl, rhs, moved)

        @pl.loop(0, hyps)
        def _(h):
            add_columns(h, first, times, vel, col_main, col_rim, bands, moved, acc)

    @pl.loop(0, hyps)
    def _(h):
        sums = acc[h]
        out[h] = (sums[:, :ROWS] / jnp.sqrt(sums[:, ROWS:])).T


def shards(science, inv_variance, psf_taps, epoch_times, velocities):
    hyps = velocities.shape[0]
    vmem = pl.BlockSpec(memory_space=pltpu.VMEM)
    smem = pl.BlockSpec(memory_space=pltpu.SMEM)
    depth = GROUP * SPAN
    return pl.pallas_call(
        functools.partial(kernel, hyps),
        out_shape=jax.ShapeDtypeStruct((hyps, ROWS, COLS), F32),
        in_specs=[smem, smem, smem, vmem, vmem, vmem],
        out_specs=vmem,
        scratch_shapes=[
            pltpu.VMEM((EPOCHS, 3, SPAN, 128), BF16),
            pltpu.VMEM((2, ROWS + 2 * EDGE, COLS), F32),
            pltpu.VMEM((3, COLS + 2 * EDGE, 128), F32),
            pltpu.VMEM((FRACS, 2, 320, 128), F32),
            pltpu.VMEM((FRACS, 320, 128), F32),
            pltpu.VMEM((FRACS, 256, 128), F32),
            pltpu.VMEM((256, hyps * ROWS), BF16),
            pltpu.VMEM((hyps, depth, 256), BF16),
            pltpu.VMEM((COLS, depth), BF16),
            pltpu.VMEM((hyps, COLS, 256), F32),
            pltpu.SemaphoreType.DMA((3,)),
            pltpu.SemaphoreType.DMA((3,)),
            pltpu.SemaphoreType.DMA((48,)),
            pltpu.SemaphoreType.DMA((EPOCHS, 2)),
        ],
        compiler_params=pltpu.CompilerParams(collective_id=0, has_side_effects=True, vmem_limit_bytes=56 << 20),
    )(epoch_times, velocities, jnp.asarray(spline_table()), psf_taps, science, inv_variance)


def solution(mesh):
    in_specs = (P("ea", "tx", "ty"), P("ea", "tx", "ty"), P("ea", None), P(), P("ea", None))
    out_specs = P("ea", "tx", "ty")
    return jax.shard_map(shards, mesh=mesh, in_specs=in_specs, out_specs=out_specs, check_vma=False)
```

```python
import functools

import jax
import jax.numpy as jnp
import numpy as np
from jax import lax
from jax.experimental import pallas as pl
from jax.experimental.pallas import tpu as pltpu
from jax.sharding import PartitionSpec as P

MESH = pl.DeviceIdType.MESH
F32 = jnp.float32
BF16 = jnp.bfloat16
ROWS, COLS = 128, 256
HALO = 32
EDGE = 40
TAPS = 9
SPAN = COLS + HALO
EPOCHS = 32
GROUP = 8
FRACS = 16
HALF = SPAN // 2


def spline_table():
    frac = np.arange(FRACS, dtype=np.float32) / np.float32(16.0)
    frac2 = frac * frac
    frac3 = frac2 * frac
    one = np.float32(1.0)
    table = np.stack(
        [
            (one - frac) ** 3 / 6,
            (3 * frac3 - 6 * frac2 + 4) / 6,
            (-3 * frac3 + 3 * frac2 + 3 * frac + 1) / 6,
            frac3 / 6,
        ],
        -1,
    )
    return table.astype(np.float32).astype(BF16).astype(np.float32)


def shift_of(speed, time):
    moved = lax.shift_right_arithmetic(speed * time, 3)
    return lax.shift_right_arithmetic(moved, 4), lax.bitwise_and(moved, 15)


def band(offset, weights):
    out = jnp.zeros(offset.shape, F32)
    for a in range(4):
        out = jnp.where(offset == a, weights[a], out)
    return out


def build_templates(wtab, ty, col_main, col_rim, row_tmpl):
    k = lax.broadcasted_iota(jnp.int32, (320, 128), 1)
    u = lax.broadcasted_iota(jnp.int32, (320, 128), 0)
    main_offset = k - u + 33
    k2 = lax.broadcasted_iota(jnp.int32, (320, 128), 1) % 32 + jnp.where(ty == 0, COLS, -HALO)
    u2 = lax.broadcasted_iota(jnp.int32, (320, 128), 0)
    rim_offset = k2 - u2 + 33
    v = lax.broadcasted_iota(jnp.int32, (256, 128), 0)
    r = lax.broadcasted_iota(jnp.int32, (256, 128), 1)
    row_offset = v - 64 - r + 1

    @pl.loop(0, FRACS)
    def _(f):
        weights = [wtab[f, a] for a in range(4)]
        col_main[f, 0] = band(main_offset, weights)
        col_main[f, 1] = band(main_offset + 128, weights)
        col_rim[f] = band(rim_offset, weights)
        row_tmpl[f] = band(row_offset, weights)


def move_rows(epoch, place, times, vel, hyps, images, row_tmpl, rhs, moved):
    time = times[epoch]
    for h in range(hyps):
        whole, frac = shift_of(vel[h, 0], time)
        lanes = slice(h * ROWS, (h + 1) * ROWS)
        rhs[0:128, lanes] = row_tmpl[frac, pl.ds(64 - whole, 128), :].astype(BF16)
        rhs[128:160, lanes] = row_tmpl[frac, pl.ds(32 - whole, 32), :].astype(BF16)
        rhs[160:192, lanes] = row_tmpl[frac, pl.ds(192 - whole, 32), :].astype(BF16)
    rims = images[epoch, 2]
    swapped = jnp.concatenate([rims[:, 64:], rims[:, :64]], axis=1)
    left = (
        jnp.concatenate([images[epoch, 0], rims], axis=1),
        jnp.concatenate([images[epoch, 1], swapped], axis=1),
    )
    for pair in range(hyps // 2):
        right = rhs[:, pair * 256 : (pair + 1) * 256]
        for i in range(2):
            res = jnp.dot(left[i], right, preferred_element_type=F32).astype(BF16)
            for q in range(2):
                h = 2 * pair + q
                part = res[:, q * ROWS : (q + 1) * ROWS]
                main = pl.multiple_of(place * COLS, COLS)
                rim = pl.multiple_of(GROUP * COLS + place * HALO, HALO)
                moved[h, pl.ds(main, COLS), i * ROWS : (i + 1) * ROWS] = part[:COLS]
                moved[h, pl.ds(rim, HALO), i * ROWS : (i + 1) * ROWS] = part[COLS:]


def add_columns(h, first, times, vel, col_main, col_rim, moved, acc):
    shifts = [shift_of(vel[h, 1], times[first + p]) for p in range(GROUP)]
    tiles = []
    for p in range(GROUP):
        whole, frac = shifts[p]
        for q in range(2):
            tiles.append(col_main[frac, q, pl.ds(32 + whole, COLS), :].astype(BF16))
    group_of_lane = lax.broadcasted_iota(jnp.int32, (COLS, 128), 1) // 32
    for q in range(GROUP // 4):
        tile = None
        for p in range(4):
            whole, frac = shifts[4 * q + p]
            rows = col_rim[frac, pl.ds(32 + whole, COLS), :]
            tile = rows if tile is None else jnp.where(group_of_lane == p, rows, tile)
        tiles.append(tile.astype(BF16))
    acc[h] += jnp.dot(jnp.concatenate(tiles, axis=1), moved[h], preferred_element_type=F32)


def kernel(
    hyps,
    times,
    vel,
    wtab,
    taps,
    science,
    inv_variance,
    out,
    images,
    raw,
    turned,
    col_main,
    col_rim,
    row_tmpl,
    rhs,
    moved,
    acc,
    edge_send,
    edge_recv,
    send_sems,
    recv_sems,
):
    tx, ty, me = lax.axis_index("tx"), lax.axis_index("ty"), lax.axis_index("ea")
    core, x, z = lax.rem(me, 2), lax.rem(lax.div(me, 2), 4), lax.div(me, 8)

    def ident(dz, dx, other=False):
        c = 1 - core if other else core
        return lax.rem(z + dz, 4) * 8 + lax.rem(x + dx, 4) * 2 + c

    up, down = {"tx": lax.rem(tx + 3, 4)}, {"tx": lax.rem(tx + 1, 4)}
    beside = {"ty": 1 - ty}
    z_up, z_down = {"ea": ident(1, 0)}, {"ea": ident(3, 0)}
    x_up, x_down = {"ea": ident(0, 1)}, {"ea": ident(0, 3)}
    twin = {"ea": ident(0, 0, True)}

    barrier = pltpu.get_barrier_semaphore()
    for peer in (up, down, beside, z_up, z_down, x_up, x_down, twin):
        pl.semaphore_signal(barrier, inc=1, device_id=peer, device_id_type=MESH)

    ivar = inv_variance[0]
    raw[0, EDGE : EDGE + ROWS] = science[0] * ivar
    raw[1, EDGE : EDGE + ROWS] = ivar
    pl.semaphore_wait(barrier, 8)

    def edge_copy(src, dst, n, peer):
        return pltpu.make_async_remote_copy(
            src_ref=src, dst_ref=dst, send_sem=edge_send.at[n], recv_sem=edge_recv.at[n], device_id=peer, device_id_type=MESH
        )

    to_up = edge_copy(raw.at[:, EDGE : 2 * EDGE], raw.at[:, EDGE + ROWS : 2 * EDGE + ROWS], 0, up)
    to_down = edge_copy(raw.at[:, ROWS : ROWS + EDGE], raw.at[:, 0:EDGE], 1, down)
    to_up.start()
    to_down.start()

    build_templates(wtab, ty, col_main, col_rim, row_tmpl)
    rhs[:, 192:256] = jnp.zeros((2, 64, hyps * ROWS), BF16)
    acc[...] = jnp.zeros_like(acc)

    tap_p = taps[...] / jnp.sum(taps[...], axis=1, keepdims=True)
    tap_q = tap_p * tap_p

    def tap(which, t):
        return (tap_p, tap_q)[which][0:1, t : t + 1]

    to_up.wait()
    to_down.wait()
    for i in range(2):
        raw[i, 0:EDGE] = jnp.where(tx == 0, 0.0, raw[i, 0:EDGE])
        raw[i, EDGE + ROWS :] = jnp.where(tx == 3, 0.0, raw[i, EDGE + ROWS :])

    def row_blur(i, start, size):
        total = None
        for t in range(TAPS):
            term = tap(i, t) * raw[i, start + t - 4 : start + t - 4 + size]
            total = term if total is None else total + term
        return total

    far = jnp.where(ty == 0, 0, EDGE + COLS)
    near = jnp.where(ty == 0, EDGE + COLS, 0)
    rims = []
    for i in range(2):
        turned[i, EDGE : EDGE + COLS] = row_blur(i, EDGE, ROWS).T
        rims.append(jnp.where(tx == 0, 0.0, row_blur(i, EDGE - HALO, HALO)))
        rims.append(jnp.where(tx == 3, 0.0, row_blur(i, EDGE + ROWS, HALO)))
    turned[2, EDGE : EDGE + COLS] = jnp.concatenate(rims, axis=0).T
    turned[:, pl.ds(pl.multiple_of(far, 8), EDGE), :] = jnp.zeros((3, EDGE, 128), F32)
    to_beside = edge_copy(
        turned.at[:, pl.ds(pl.multiple_of(EDGE + jnp.where(ty == 0, COLS - EDGE, 0), 8), EDGE), :],
        turned.at[:, pl.ds(pl.multiple_of(far, 8), EDGE), :],
        2,
        beside,
    )
    to_beside.start()
    to_beside.wait()

    lane = lax.broadcasted_iota(jnp.int32, (1, 128), 1)

    def col_tap(b, t):
        if b < 2:
            return tap(b, t)
        return jnp.where(lane < 64, tap(0, t), tap(1, t))

    rim_start = jnp.where(ty == 0, EDGE + COLS, EDGE - HALO)
    for b in range(3):
        total, rim = None, None
        for t in range(TAPS):
            term = col_tap(b, t) * turned[b, EDGE + t - 4 : EDGE + t - 4 + COLS]
            total = term if total is None else total + term
            term = col_tap(b, t) * turned[b, pl.ds(rim_start + t - 4, HALO), :]
            rim = term if rim is None else rim + term
        images[me, b, 0:COLS] = total.astype(BF16)
        images[me, b, COLS:SPAN] = rim.astype(BF16)

    sends = []

    def view(block, part):
        if part is None:
            return images.at[block]
        return images.at[block, :, part * HALF : (part + 1) * HALF]

    def descriptor(block, part, peer, n):
        return pltpu.make_async_remote_copy(
            src_ref=view(block, part),
            dst_ref=view(block, part),
            send_sem=send_sems.at[n],
            recv_sem=recv_sems.at[block, 0 if part is None else part],
            device_id=peer,
            device_id_type=MESH,
        )

    def send(block, part, peer):
        descriptor(block, part, peer, len(sends)).start()
        sends.append((block, part, peer))

    def arrived(block, part=None):
        descriptor(block, part, twin, 0).wait_recv()

    own = ident(0, 0)
    for peer in (z_up, z_down, x_up, x_down, twin):
        send(own, None, peer)

    ids = {(dz, dx): ident(dz, dx) for dz in range(4) for dx in range(4)}

    def x_arrivals(dz, forward):
        below, above = ids[dz, 3], ids[dz, 1]
        arrived(below)
        if forward:
            send(below, 0, x_up)
        send(below, None, twin)
        arrived(above)
        if forward:
            send(above, 1, x_down)
        send(above, None, twin)

    def spread(block):
        for peer in (x_up, x_down, twin):
            send(block, None, peer)

    def halves_arrived(block):
        arrived(block, 0)
        arrived(block, 1)

    def start_rows():
        x_arrivals(0, True)

    def own_across():
        across = ids[0, 2]
        halves_arrived(across)
        for peer in (twin, z_up, z_down):
            send(across, None, peer)

    def z_neighbours():
        low, high = ids[3, 0], ids[1, 0]
        arrived(low)
        send(low, 0, z_up)
        spread(low)
        arrived(high)
        send(high, 1, z_down)
        spread(high)

    def z_opposite():
        opposite = ids[2, 0]
        halves_arrived(opposite)
        spread(opposite)

    def z_across(dz):
        across = ids[dz, 2]
        arrived(across)
        send(across, None, twin)

    def last_across():
        across = ids[2, 2]
        halves_arrived(across)
        send(across, None, twin)

    duties = {
        (0, 1): [start_rows],
        (0, 3): [own_across],
        (0, 4): [z_neighbours],
        (0, 6): [z_opposite],
        (1, 1): [lambda: x_arrivals(3, False)],
        (1, 3): [lambda: z_across(3)],
        (1, 4): [lambda: x_arrivals(1, False)],
        (1, 6): [lambda: z_across(1)],
        (2, 2): [lambda: x_arrivals(2, True)],
        (2, 5): [last_across],
    }
    steps = 7

    def attend(g, step, only):
        for (group, at), acts in duties.items():
            if at in only:

                @pl.when(jnp.logical_and(g == group, step == at))
                def _(acts=acts):
                    for act in acts:
                        act()

    @pl.loop(0, EPOCHS // GROUP)
    def _(g):
        dz = jnp.where(g == 0, 0, jnp.where(g == 1, 3, jnp.where(g == 2, 1, 2)))
        first = lax.rem(z + dz, 4) * GROUP

        @pl.loop(0, 4)
        def _(j):
            attend(g, j, range(4))
            dx = jnp.where(j == 0, 0, jnp.where(j == 1, 3, jnp.where(j == 2, 1, 2)))
            mine, other = ident(dz, dx), ident(dz, dx, True)
            arrived(other)
            for n, block in enumerate((mine, other)):
                move_rows(block, lax.rem(block, GROUP), times, vel, hyps, images, row_tmpl, rhs.at[n], moved)

        @pl.loop(0, hyps // 2)
        def _(pair):
            attend(g, pair + 4, range(4, steps))
            for n in range(2):
                add_columns(2 * pair + n, first, times, vel, col_main, col_rim, moved, acc)

    for n, (block, part, peer) in enumerate(sends):
        descriptor(block, part, peer, n).wait_send()

    @pl.loop(0, hyps)
    def _(h):
        sums = acc[h]
        out[h] = (sums[:, :ROWS] / jnp.sqrt(sums[:, ROWS:])).T


def shards(science, inv_variance, psf_taps, epoch_times, velocities):
    hyps = velocities.shape[0]
    vmem = pl.BlockSpec(memory_space=pltpu.VMEM)
    smem = pl.BlockSpec(memory_space=pltpu.SMEM)
    depth = GROUP * SPAN
    return pl.pallas_call(
        functools.partial(kernel, hyps),
        out_shape=jax.ShapeDtypeStruct((hyps, ROWS, COLS), F32),
        in_specs=[smem, smem, smem, vmem, vmem, vmem],
        out_specs=vmem,
        scratch_shapes=[
            pltpu.VMEM((EPOCHS, 3, SPAN, 128), BF16),
            pltpu.VMEM((2, ROWS + 2 * EDGE, COLS), F32),
            pltpu.VMEM((3, COLS + 2 * EDGE, 128), F32),
            pltpu.VMEM((FRACS, 2, 320, 128), F32),
            pltpu.VMEM((FRACS, 320, 128), F32),
            pltpu.VMEM((FRACS, 256, 128), F32),
            pltpu.VMEM((2, 256, hyps * ROWS), BF16),
            pltpu.VMEM((hyps, depth, 256), BF16),
            pltpu.VMEM((hyps, COLS, 256), F32),
            pltpu.SemaphoreType.DMA((3,)),
            pltpu.SemaphoreType.DMA((3,)),
            pltpu.SemaphoreType.DMA((48,)),
            pltpu.SemaphoreType.DMA((EPOCHS, 2)),
        ],
        compiler_params=pltpu.CompilerParams(collective_id=0, has_side_effects=True, vmem_limit_bytes=56 << 20),
    )(epoch_times, velocities, jnp.asarray(spline_table()), psf_taps, science, inv_variance)


def solution(mesh):
    in_specs = (P("ea", "tx", "ty"), P("ea", "tx", "ty"), P("ea", None), P(), P("ea", None))
    out_specs = P("ea", "tx", "ty")
    return jax.shard_map(shards, mesh=mesh, in_specs=in_specs, out_specs=out_specs, check_vma=False)
```

```python
import functools

import jax
import jax.numpy as jnp
import numpy as np
from jax import lax
from jax.experimental import pallas as pl
from jax.experimental.pallas import tpu as pltpu
from jax.sharding import PartitionSpec as P

MESH = pl.DeviceIdType.MESH
F32 = jnp.float32
BF16 = jnp.bfloat16
ROWS, COLS = 128, 256
HALO = 32
EDGE = 40
TAPS = 9
SPAN = COLS + HALO
EPOCHS = 32
GROUP = 8
FRACS = 16
HALF = SPAN // 2


def spline_table():
    frac = np.arange(FRACS, dtype=np.float32) / np.float32(16.0)
    frac2 = frac * frac
    frac3 = frac2 * frac
    one = np.float32(1.0)
    table = np.stack(
        [
            (one - frac) ** 3 / 6,
            (3 * frac3 - 6 * frac2 + 4) / 6,
            (-3 * frac3 + 3 * frac2 + 3 * frac + 1) / 6,
            frac3 / 6,
        ],
        -1,
    )
    return table.astype(np.float32).astype(BF16).astype(np.float32)


def shift_of(speed, time):
    moved = lax.shift_right_arithmetic(speed * time, 3)
    return lax.shift_right_arithmetic(moved, 4), lax.bitwise_and(moved, 15)


def band(offset, weights):
    out = jnp.zeros(offset.shape, F32)
    for a in range(4):
        out = jnp.where(offset == a, weights[a], out)
    return out


def build_templates(wtab, ty, col_main, col_rim, row_tmpl):
    k = lax.broadcasted_iota(jnp.int32, (320, 128), 1)
    u = lax.broadcasted_iota(jnp.int32, (320, 128), 0)
    main_offset = k - u + 33
    k2 = lax.broadcasted_iota(jnp.int32, (320, 128), 1) % 32 + jnp.where(ty == 0, COLS, -HALO)
    u2 = lax.broadcasted_iota(jnp.int32, (320, 128), 0)
    rim_offset = k2 - u2 + 33
    v = lax.broadcasted_iota(jnp.int32, (256, 128), 0)
    r = lax.broadcasted_iota(jnp.int32, (256, 128), 1)
    row_offset = v - 64 - r + 1

    @pl.loop(0, FRACS)
    def _(f):
        weights = [wtab[f, a] for a in range(4)]
        col_main[f, 0] = band(main_offset, weights)
        col_main[f, 1] = band(main_offset + 128, weights)
        col_rim[f] = band(rim_offset, weights)
        row_tmpl[f] = band(row_offset, weights)


def move_rows(epoch, time, place, ty, vel, hyps, images, row_tmpl, rhs, moved):
    for h in range(hyps):
        whole, frac = shift_of(vel[0, h], time)
        lanes = slice(h * ROWS, (h + 1) * ROWS)
        rhs[0:128, lanes] = row_tmpl[frac, pl.ds(64 - whole, 128), :].astype(BF16)
        rhs[128:160, lanes] = row_tmpl[frac, pl.ds(32 - whole, 32), :].astype(BF16)
        rhs[160:192, lanes] = row_tmpl[frac, pl.ds(192 - whole, 32), :].astype(BF16)
    main_at = pl.multiple_of(jnp.where(ty == 0, 0, HALO), HALO)
    rim_at = pl.multiple_of(jnp.where(ty == 0, COLS, 0), HALO)
    planes = [
        jnp.concatenate([images[epoch, b, pl.ds(main_at, COLS), :], images[epoch, b, pl.ds(rim_at, HALO), :]], axis=0)
        for b in range(3)
    ]
    swapped = jnp.concatenate([planes[2][:, 64:], planes[2][:, :64]], axis=1)
    left = (
        jnp.concatenate([planes[0], planes[2]], axis=1),
        jnp.concatenate([planes[1], swapped], axis=1),
    )
    for pair in range(hyps // 2):
        right = rhs[:, pair * 256 : (pair + 1) * 256]
        for i in range(2):
            res = jnp.dot(left[i], right, preferred_element_type=F32).astype(BF16)
            for q in range(2):
                h = 2 * pair + q
                part = res[:, q * ROWS : (q + 1) * ROWS]
                main = pl.multiple_of(place * COLS, COLS)
                rim = pl.multiple_of(GROUP * COLS + place * HALO, HALO)
                moved[h, pl.ds(main, COLS), i * ROWS : (i + 1) * ROWS] = part[:COLS]
                moved[h, pl.ds(rim, HALO), i * ROWS : (i + 1) * ROWS] = part[COLS:]


def add_columns(h, first, times, vel, col_main, col_rim, moved, acc):
    shifts = [shift_of(vel[1, h], times[first + p]) for p in range(GROUP)]
    tiles = []
    for p in range(GROUP):
        whole, frac = shifts[p]
        for q in range(2):
            tiles.append(col_main[frac, q, pl.ds(32 + whole, COLS), :].astype(BF16))
    group_of_lane = lax.broadcasted_iota(jnp.int32, (COLS, 128), 1) // 32
    for q in range(GROUP // 4):
        tile = None
        for p in range(4):
            whole, frac = shifts[4 * q + p]
            rows = col_rim[frac, pl.ds(32 + whole, COLS), :]
            tile = rows if tile is None else jnp.where(group_of_lane == p, rows, tile)
        tiles.append(tile.astype(BF16))
    acc[h] += jnp.dot(jnp.concatenate(tiles, axis=1), moved[h], preferred_element_type=F32)


def kernel(
    hyps,
    times,
    vel,
    wtab,
    taps,
    science,
    inv_variance,
    out,
    images,
    raw,
    turned,
    col_main,
    col_rim,
    row_tmpl,
    rhs,
    moved,
    acc,
    when,
    edge_send,
    edge_recv,
    send_sems,
    recv_sems,
):
    tx, ty, me = lax.axis_index("tx"), lax.axis_index("ty"), lax.axis_index("ea")
    core, x, z = lax.rem(me, 2), lax.rem(lax.div(me, 2), 4), lax.div(me, 8)

    def ident(dz, dx, other=0):
        return lax.rem(z + dz, 4) * 8 + lax.rem(x + dx, 4) * 2 + lax.rem(core + other, 2)

    up, down = {"tx": lax.rem(tx + 3, 4)}, {"tx": lax.rem(tx + 1, 4)}
    beside = {"ty": 1 - ty}
    z_up, z_down = {"ea": ident(1, 0)}, {"ea": ident(3, 0)}
    x_up, x_down = {"ea": ident(0, 1)}, {"ea": ident(0, 3)}
    twin = {"ea": ident(0, 0, 1)}

    barrier = pltpu.get_barrier_semaphore()
    for peer in (up, down, beside, z_up, z_down, x_up, x_down, twin):
        pl.semaphore_signal(barrier, inc=1, device_id=peer, device_id_type=MESH)

    ivar = inv_variance[0]
    raw[0, EDGE : EDGE + ROWS] = science[0] * ivar
    raw[1, EDGE : EDGE + ROWS] = ivar
    pl.semaphore_wait(barrier, 8)

    def edge_copy(src, dst, n, peer):
        return pltpu.make_async_remote_copy(
            src_ref=src, dst_ref=dst, send_sem=edge_send.at[n], recv_sem=edge_recv.at[n], device_id=peer, device_id_type=MESH
        )

    to_up = edge_copy(raw.at[:, EDGE : 2 * EDGE], raw.at[:, EDGE + ROWS : 2 * EDGE + ROWS], 0, up)
    to_down = edge_copy(raw.at[:, ROWS : ROWS + EDGE], raw.at[:, 0:EDGE], 1, down)
    to_up.start()
    to_down.start()

    build_templates(wtab, ty, col_main, col_rim, row_tmpl)
    rhs[:, 192:256] = jnp.zeros((2, 64, hyps * ROWS), BF16)
    acc[...] = jnp.zeros_like(acc)

    tap_p = taps[...] / jnp.sum(taps[...], axis=1, keepdims=True)
    tap_q = tap_p * tap_p

    def tap(which, t):
        return (tap_p, tap_q)[which][0:1, t : t + 1]

    to_up.wait()
    to_down.wait()
    for i in range(2):
        raw[i, 0:EDGE] = jnp.where(tx == 0, 0.0, raw[i, 0:EDGE])
        raw[i, EDGE + ROWS :] = jnp.where(tx == 3, 0.0, raw[i, EDGE + ROWS :])

    def row_blur(i, start, size):
        total = None
        for t in range(TAPS):
            term = tap(i, t) * raw[i, start + t - 4 : start + t - 4 + size]
            total = term if total is None else total + term
        return total

    far = jnp.where(ty == 0, 0, EDGE + COLS)
    near = jnp.where(ty == 0, EDGE + COLS, 0)
    rims = []
    for i in range(2):
        turned[i, EDGE : EDGE + COLS] = row_blur(i, EDGE, ROWS).T
        rims.append(jnp.where(tx == 0, 0.0, row_blur(i, EDGE - HALO, HALO)))
        rims.append(jnp.where(tx == 3, 0.0, row_blur(i, EDGE + ROWS, HALO)))
    turned[2, EDGE : EDGE + COLS] = jnp.concatenate(rims, axis=0).T
    turned[:, pl.ds(pl.multiple_of(far, 8), EDGE), :] = jnp.zeros((3, EDGE, 128), F32)
    to_beside = edge_copy(
        turned.at[:, pl.ds(pl.multiple_of(EDGE + jnp.where(ty == 0, COLS - EDGE, 0), 8), EDGE), :],
        turned.at[:, pl.ds(pl.multiple_of(far, 8), EDGE), :],
        2,
        beside,
    )
    to_beside.start()

    lane = lax.broadcasted_iota(jnp.int32, (1, 128), 1)

    def col_tap(b, t):
        if b < 2:
            return tap(b, t)
        return jnp.where(lane < 64, tap(0, t), tap(1, t))

    base = jnp.where(ty == 0, EDGE, EDGE - HALO)
    part_at = [pl.multiple_of(HALF * (ty if part == 0 else 1 - ty), 16) for part in range(2)]

    def col_blur(part):
        for b in range(3):
            total = None
            for t in range(TAPS):
                term = col_tap(b, t) * turned[b, pl.ds(base + part_at[part] + t - 4, HALF), :]
                total = term if total is None else total + term
            images[me, b, pl.ds(part_at[part], HALF), :] = total.astype(BF16)

    sends = []
    ids = {(dz, dx): ident(dz, dx) for dz in range(4) for dx in range(4)}
    below, above, own = ids[0, 3], ids[0, 1], ids[0, 0]
    low, high, opposite = ids[3, 0], ids[1, 0], ids[2, 0]

    def descriptor(block, part, peer, n):
        view = images.at[block] if part is None else images.at[block, :, pl.ds(part_at[part], HALF)]
        return pltpu.make_async_remote_copy(
            src_ref=view,
            dst_ref=view,
            send_sem=send_sems.at[n],
            recv_sem=recv_sems.at[block, 0 if part is None else part],
            device_id=peer,
            device_id_type=MESH,
        )

    def send(block, part, *peers):
        for peer in peers:
            descriptor(block, part, peer, len(sends)).start()
            sends.append((block, part, peer))

    def arrived(block, part=None):
        descriptor(block, part, twin, 0).wait_recv()

    col_blur(0)
    send(own, 0, z_up, z_down, x_up, x_down)
    to_beside.wait()
    col_blur(1)
    send(own, 1, z_down, z_up, x_down, x_up)
    send(own, None, twin)

    def first_x():
        arrived(below, 0)
        send(below, 0, x_up)
        arrived(above, 0)

    def second_x():
        arrived(above, 1)
        send(above, 1, x_down)
        arrived(below, 1)
        send(below, None, twin)
        send(above, None, twin)

    def first_z():
        arrived(low, 0)
        send(low, 0, z_up, x_up, x_down)
        arrived(high, 0)
        send(high, 0, x_up, x_down)

    def own_across():
        across = ids[0, 2]
        arrived(across, 0)
        arrived(across, 1)
        send(across, None, twin)

    def second_z():
        arrived(high, 1)
        send(high, 1, z_down, x_up, x_down)
        arrived(low, 1)
        send(low, 1, x_up, x_down)
        send(low, None, twin)
        send(high, None, twin)

    def z_opposite():
        for part in range(2):
            arrived(opposite, part)
            send(opposite, part, x_up, x_down)
        for part in range(2):
            send(ids[0, 2], part, z_up, z_down)
        send(opposite, None, twin)

    def x_arrivals(dz):
        for dx in (3, 1):
            arrived(ids[dz, dx], 0)
            arrived(ids[dz, dx], 1)
            send(ids[dz, dx], None, twin)

    def across_arrives(dz):
        arrived(ids[dz, 2], 0)
        arrived(ids[dz, 2], 1)
        send(ids[dz, 2], None, twin)

    def last_x(part):
        arrived(ids[2, 3], part)
        arrived(ids[2, 1], part)
        if part == 0:
            send(ids[2, 3], 0, x_up)
        else:
            send(ids[2, 1], 1, x_down)
            send(ids[2, 3], None, twin)
            send(ids[2, 1], None, twin)

    duties = {
        (0, 1): [first_x, first_z, second_x],
        (0, 3): [own_across],
        (0, 4): [second_z],
        (1, 0): [z_opposite],
        (1, 2): [lambda: x_arrivals(3)],
        (1, 4): [lambda: x_arrivals(1)],
        (1, 5): [lambda: last_x(0)],
        (2, 1): [lambda: last_x(1)],
        (2, 4): [lambda: across_arrives(3), lambda: across_arrives(1)],
        (2, 6): [lambda: across_arrives(2)],
    }
    steps = 7

    def attend(g, step, only):
        for (group, at), acts in duties.items():
            if at in only:

                @pl.when(jnp.logical_and(g == group, step == at))
                def _(acts=acts):
                    for act in acts:
                        act()

    def pick(index, values):
        out = values[-1]
        for n in range(len(values) - 2, -1, -1):
            out = jnp.where(index == n, values[n], out)
        return out

    order = [
        ((0, 0, 0), (0, 0, 1)),
        ((0, 3, 0), (0, 1, 0)),
        ((0, 3, 1), (0, 1, 1)),
        ((0, 2, 0), (0, 2, 1)),
        ((3, 0, 0), (1, 0, 0)),
        ((3, 0, 1), (1, 0, 1)),
        ((3, 3, 0), (3, 1, 0)),
        ((3, 3, 1), (3, 1, 1)),
        ((1, 3, 0), (1, 1, 0)),
        ((1, 3, 1), (1, 1, 1)),
        ((2, 0, 0), (2, 0, 1)),
        ((2, 3, 0), (2, 1, 0)),
        ((2, 3, 1), (2, 1, 1)),
        ((3, 2, 0), (1, 2, 0)),
        ((3, 2, 1), (1, 2, 1)),
        ((2, 2, 0), (2, 2, 1)),
    ]
    for n, pair in enumerate(order):
        for m, spot in enumerate(pair):
            when[2 * n + m] = times[ident(*spot)]

    @pl.loop(0, EPOCHS // GROUP)
    def _(g):
        @pl.loop(0, 4)
        def _(j):
            attend(g, j, range(4))
            step = 4 * g + j
            blocks = []
            for m in range(2):
                dz, dx, other = [pick(step, [pair[m][axis] for pair in order]) for axis in range(3)]
                blocks.append(ident(dz, dx, other))

                @pl.when(other == 1)
                def _():
                    arrived(blocks[m])

            for m, block in enumerate(blocks):
                move_rows(
                    block, when[2 * step + m], 2 * j + m, ty, vel, hyps, images, row_tmpl, rhs.at[m], moved
                )

        @pl.loop(0, hyps // 2)
        def _(pair):
            attend(g, pair + 4, range(4, steps))
            for n in range(2):
                add_columns(2 * pair + n, g * GROUP, when, vel, col_main, col_rim, moved, acc)

    for n, (block, part, peer) in enumerate(sends):
        descriptor(block, part, peer, n).wait_send()

    @pl.loop(0, hyps)
    def _(h):
        sums = acc[h]
        out[h] = (sums[:, :ROWS] / jnp.sqrt(sums[:, ROWS:])).T


def shards(science, inv_variance, psf_taps, epoch_times, velocities):
    hyps = velocities.shape[0]
    vmem = pl.BlockSpec(memory_space=pltpu.VMEM)
    smem = pl.BlockSpec(memory_space=pltpu.SMEM)
    depth = GROUP * SPAN
    return pl.pallas_call(
        functools.partial(kernel, hyps),
        out_shape=jax.ShapeDtypeStruct((hyps, ROWS, COLS), F32),
        in_specs=[smem, smem, smem, vmem, vmem, vmem],
        out_specs=vmem,
        scratch_shapes=[
            pltpu.VMEM((EPOCHS, 3, SPAN, 128), BF16),
            pltpu.VMEM((2, ROWS + 2 * EDGE, COLS), F32),
            pltpu.VMEM((3, COLS + 2 * EDGE, 128), F32),
            pltpu.VMEM((FRACS, 2, 320, 128), F32),
            pltpu.VMEM((FRACS, 320, 128), F32),
            pltpu.VMEM((FRACS, 256, 128), F32),
            pltpu.VMEM((2, 256, hyps * ROWS), BF16),
            pltpu.VMEM((hyps, depth, 256), BF16),
            pltpu.VMEM((hyps, COLS, 256), F32),
            pltpu.SMEM((EPOCHS,), jnp.int32),
            pltpu.SemaphoreType.DMA((3,)),
            pltpu.SemaphoreType.DMA((3,)),
            pltpu.SemaphoreType.DMA((64,)),
            pltpu.SemaphoreType.DMA((EPOCHS, 2)),
        ],
        compiler_params=pltpu.CompilerParams(collective_id=0, has_side_effects=True, vmem_limit_bytes=56 << 20),
    )(epoch_times, velocities.T, jnp.asarray(spline_table()), psf_taps, science, inv_variance)


def solution(mesh):
    in_specs = (P("ea", "tx", "ty"), P("ea", "tx", "ty"), P("ea", None), P(), P("ea", None))
    out_specs = P("ea", "tx", "ty")
    return jax.shard_map(shards, mesh=mesh, in_specs=in_specs, out_specs=out_specs, check_vma=False)
```

```python
import functools

import jax
import jax.numpy as jnp
import numpy as np
from jax import lax
from jax.experimental import pallas as pl
from jax.experimental.pallas import tpu as pltpu
from jax.sharding import PartitionSpec as P

MESH = pl.DeviceIdType.MESH
F32 = jnp.float32
BF16 = jnp.bfloat16
ROWS, COLS = 128, 256
HALO = 32
EDGE = 40
TAPS = 9
SPAN = COLS + HALO
EPOCHS = 32
GROUP = 8
FRACS = 16
HALF = SPAN // 2


def spline_table():
    frac = np.arange(FRACS, dtype=np.float32) / np.float32(16.0)
    frac2 = frac * frac
    frac3 = frac2 * frac
    one = np.float32(1.0)
    table = np.stack(
        [
            (one - frac) ** 3 / 6,
            (3 * frac3 - 6 * frac2 + 4) / 6,
            (-3 * frac3 + 3 * frac2 + 3 * frac + 1) / 6,
            frac3 / 6,
        ],
        -1,
    )
    return table.astype(np.float32).astype(BF16).astype(np.float32)


def shift_of(speed, time):
    moved = lax.shift_right_arithmetic(speed * time, 3)
    return lax.shift_right_arithmetic(moved, 4), lax.bitwise_and(moved, 15)


def band(offset, weights):
    out = jnp.zeros(offset.shape, F32)
    for a in range(4):
        out = jnp.where(offset == a, weights[a], out)
    return out


def build_templates(wtab, ty, col_main, col_rim, row_tmpl):
    k = lax.broadcasted_iota(jnp.int32, (320, 128), 1)
    u = lax.broadcasted_iota(jnp.int32, (320, 128), 0)
    main_offset = k - u + 33
    k2 = lax.broadcasted_iota(jnp.int32, (320, 128), 1) % 32 + jnp.where(ty == 0, COLS, -HALO)
    u2 = lax.broadcasted_iota(jnp.int32, (320, 128), 0)
    rim_offset = k2 - u2 + 33
    v = lax.broadcasted_iota(jnp.int32, (256, 128), 0)
    r = lax.broadcasted_iota(jnp.int32, (256, 128), 1)
    row_offset = v - 64 - r + 1

    @pl.loop(0, FRACS)
    def _(f):
        weights = [wtab[f, a] for a in range(4)]
        col_main[f, 0] = band(main_offset, weights)
        col_main[f, 1] = band(main_offset + 128, weights)
        col_rim[f] = band(rim_offset, weights)
        row_tmpl[f] = band(row_offset, weights)


def move_rows(epoch, time, place, ty, vel, hyps, images, row_tmpl, rhs, moved):
    for h in range(hyps):
        whole, frac = shift_of(vel[0, h], time)
        lanes = slice(h * ROWS, (h + 1) * ROWS)
        rhs[0:128, lanes] = row_tmpl[frac, pl.ds(64 - whole, 128), :].astype(BF16)
        rhs[128:160, lanes] = row_tmpl[frac, pl.ds(32 - whole, 32), :].astype(BF16)
        rhs[160:192, lanes] = row_tmpl[frac, pl.ds(192 - whole, 32), :].astype(BF16)
    main_at = pl.multiple_of(jnp.where(ty == 0, 0, HALO), HALO)
    rim_at = pl.multiple_of(jnp.where(ty == 0, COLS, 0), HALO)
    planes = [
        jnp.concatenate([images[epoch, b, pl.ds(main_at, COLS), :], images[epoch, b, pl.ds(rim_at, HALO), :]], axis=0)
        for b in range(3)
    ]
    swapped = jnp.concatenate([planes[2][:, 64:], planes[2][:, :64]], axis=1)
    left = (
        jnp.concatenate([planes[0], planes[2]], axis=1),
        jnp.concatenate([planes[1], swapped], axis=1),
    )
    for pair in range(hyps // 2):
        right = rhs[:, pair * 256 : (pair + 1) * 256]
        for i in range(2):
            res = jnp.dot(left[i], right, preferred_element_type=F32).astype(BF16)
            for q in range(2):
                h = 2 * pair + q
                part = res[:, q * ROWS : (q + 1) * ROWS]
                main = pl.multiple_of(place * COLS, COLS)
                rim = pl.multiple_of(GROUP * COLS + place * HALO, HALO)
                moved[h, pl.ds(main, COLS), i * ROWS : (i + 1) * ROWS] = part[:COLS]
                moved[h, pl.ds(rim, HALO), i * ROWS : (i + 1) * ROWS] = part[COLS:]


def add_columns(h, first, times, vel, col_main, col_rim, moved, acc):
    shifts = [shift_of(vel[1, h], times[first + p]) for p in range(GROUP)]
    tiles = []
    for p in range(GROUP):
        whole, frac = shifts[p]
        for q in range(2):
            tiles.append(col_main[frac, q, pl.ds(32 + whole, COLS), :].astype(BF16))
    group_of_lane = lax.broadcasted_iota(jnp.int32, (COLS, 128), 1) // 32
    for q in range(GROUP // 4):
        tile = None
        for p in range(4):
            whole, frac = shifts[4 * q + p]
            rows = col_rim[frac, pl.ds(32 + whole, COLS), :]
            tile = rows if tile is None else jnp.where(group_of_lane == p, rows, tile)
        tiles.append(tile.astype(BF16))
    acc[h] += jnp.dot(jnp.concatenate(tiles, axis=1), moved[h], preferred_element_type=F32)


def kernel(
    hyps,
    times,
    vel,
    wtab,
    taps,
    science,
    inv_variance,
    out,
    images,
    raw,
    turned,
    col_main,
    col_rim,
    row_tmpl,
    rhs,
    moved,
    acc,
    when,
    edge_send,
    edge_recv,
    send_sems,
    recv_sems,
):
    tx, ty, me = lax.axis_index("tx"), lax.axis_index("ty"), lax.axis_index("ea")
    core, x, z = lax.rem(me, 2), lax.rem(lax.div(me, 2), 4), lax.div(me, 8)

    def ident(dz, dx, other=0):
        return lax.rem(z + dz, 4) * 8 + lax.rem(x + dx, 4) * 2 + lax.rem(core + other, 2)

    up, down = {"tx": lax.rem(tx + 3, 4)}, {"tx": lax.rem(tx + 1, 4)}
    beside = {"ty": 1 - ty}
    z_up, z_down = {"ea": ident(1, 0)}, {"ea": ident(3, 0)}
    x_up, x_down = {"ea": ident(0, 1)}, {"ea": ident(0, 3)}
    twin = {"ea": ident(0, 0, 1)}

    barrier = pltpu.get_barrier_semaphore()
    for peer in (up, down, beside, z_up, z_down, x_up, x_down, twin):
        pl.semaphore_signal(barrier, inc=1, device_id=peer, device_id_type=MESH)

    ivar = inv_variance[0]
    raw[0, EDGE : EDGE + ROWS] = science[0] * ivar
    raw[1, EDGE : EDGE + ROWS] = ivar
    pl.semaphore_wait(barrier, 8)

    def edge_copy(src, dst, n, peer):
        return pltpu.make_async_remote_copy(
            src_ref=src, dst_ref=dst, send_sem=edge_send.at[n], recv_sem=edge_recv.at[n], device_id=peer, device_id_type=MESH
        )

    to_up = edge_copy(raw.at[:, EDGE : 2 * EDGE], raw.at[:, EDGE + ROWS : 2 * EDGE + ROWS], 0, up)
    to_down = edge_copy(raw.at[:, ROWS : ROWS + EDGE], raw.at[:, 0:EDGE], 1, down)
    to_up.start()
    to_down.start()

    build_templates(wtab, ty, col_main, col_rim, row_tmpl)
    rhs[:, 192:256] = jnp.zeros((2, 64, hyps * ROWS), BF16)
    acc[...] = jnp.zeros_like(acc)

    tap_p = taps[...] / jnp.sum(taps[...], axis=1, keepdims=True)
    tap_q = tap_p * tap_p

    def tap(which, t):
        return (tap_p, tap_q)[which][0:1, t : t + 1]

    to_up.wait()
    to_down.wait()
    for i in range(2):
        raw[i, 0:EDGE] = jnp.where(tx == 0, 0.0, raw[i, 0:EDGE])
        raw[i, EDGE + ROWS :] = jnp.where(tx == 3, 0.0, raw[i, EDGE + ROWS :])

    def row_blur(i, start, size):
        total = None
        for t in range(TAPS):
            term = tap(i, t) * raw[i, start + t - 4 : start + t - 4 + size]
            total = term if total is None else total + term
        return total

    far = jnp.where(ty == 0, 0, EDGE + COLS)
    near = jnp.where(ty == 0, EDGE + COLS, 0)
    rims = []
    for i in range(2):
        turned[i, EDGE : EDGE + COLS] = row_blur(i, EDGE, ROWS).T
        rims.append(jnp.where(tx == 0, 0.0, row_blur(i, EDGE - HALO, HALO)))
        rims.append(jnp.where(tx == 3, 0.0, row_blur(i, EDGE + ROWS, HALO)))
    turned[2, EDGE : EDGE + COLS] = jnp.concatenate(rims, axis=0).T
    turned[:, pl.ds(pl.multiple_of(far, 8), EDGE), :] = jnp.zeros((3, EDGE, 128), F32)
    to_beside = edge_copy(
        turned.at[:, pl.ds(pl.multiple_of(EDGE + jnp.where(ty == 0, COLS - EDGE, 0), 8), EDGE), :],
        turned.at[:, pl.ds(pl.multiple_of(far, 8), EDGE), :],
        2,
        beside,
    )
    to_beside.start()

    lane = lax.broadcasted_iota(jnp.int32, (1, 128), 1)

    def col_tap(b, t):
        if b < 2:
            return tap(b, t)
        return jnp.where(lane < 64, tap(0, t), tap(1, t))

    base = jnp.where(ty == 0, EDGE, EDGE - HALO)
    part_at = [pl.multiple_of(HALF * (ty if part == 0 else 1 - ty), 16) for part in range(2)]

    def col_blur(part):
        for b in range(3):
            total = None
            for t in range(TAPS):
                term = col_tap(b, t) * turned[b, pl.ds(base + part_at[part] + t - 4, HALF), :]
                total = term if total is None else total + term
            images[me, b, pl.ds(part_at[part], HALF), :] = total.astype(BF16)

    sends = []
    ids = {(dz, dx): ident(dz, dx) for dz in range(4) for dx in range(4)}
    below, above, own = ids[0, 3], ids[0, 1], ids[0, 0]
    low, high, opposite = ids[3, 0], ids[1, 0], ids[2, 0]

    def descriptor(block, part, peer, n):
        view = images.at[block] if part is None else images.at[block, :, pl.ds(part_at[part], HALF)]
        return pltpu.make_async_remote_copy(
            src_ref=view,
            dst_ref=view,
            send_sem=send_sems.at[n],
            recv_sem=recv_sems.at[block, 0 if part is None else part],
            device_id=peer,
            device_id_type=MESH,
        )

    def send(block, part, *peers):
        for peer in peers:
            descriptor(block, part, peer, len(sends)).start()
            sends.append((block, part, peer))

    def arrived(block, part=None):
        descriptor(block, part, twin, 0).wait_recv()

    col_blur(0)
    send(own, 0, z_up, z_down, x_up, x_down)
    to_beside.wait()
    col_blur(1)
    send(own, 1, z_down, z_up, x_down, x_up)
    send(own, None, twin)

    def first_x():
        arrived(below, 0)
        send(below, 0, x_up)
        arrived(above, 0)

    def second_x():
        arrived(above, 1)
        send(above, 1, x_down)
        arrived(below, 1)
        send(below, None, twin)
        send(above, None, twin)

    def first_z():
        arrived(low, 0)
        send(low, 0, z_up, x_up, x_down)
        arrived(high, 0)
        send(high, 0, x_up, x_down)

    def own_across():
        across = ids[0, 2]
        arrived(across, 0)
        arrived(across, 1)
        send(across, None, twin)

    def second_z():
        arrived(high, 1)
        send(high, 1, z_down, x_up, x_down)
        arrived(low, 1)
        send(low, 1, x_up, x_down)
        send(low, None, twin)
        send(high, None, twin)

    def z_opposite(part):
        arrived(opposite, part)
        send(opposite, part, x_up, x_down)
        if part == 1:
            send(ids[0, 2], 0, z_up, z_down)
            send(ids[0, 2], 1, z_up, z_down)
            send(opposite, None, twin)

    def x_arrivals(dz):
        for dx in (3, 1):
            arrived(ids[dz, dx], 0)
            arrived(ids[dz, dx], 1)
            send(ids[dz, dx], None, twin)

    def across_arrives(dz):
        arrived(ids[dz, 2], 0)
        arrived(ids[dz, 2], 1)
        send(ids[dz, 2], None, twin)

    def last_x(part):
        arrived(ids[2, 3], part)
        arrived(ids[2, 1], part)
        if part == 0:
            send(ids[2, 3], 0, x_up)
        else:
            send(ids[2, 1], 1, x_down)
            send(ids[2, 3], None, twin)
            send(ids[2, 1], None, twin)

    duties = {
        (0, 1): [first_x, first_z, second_x],
        (0, 3): [second_z],
        (0, 4): [own_across],
        (0, 5): [lambda: z_opposite(0)],
        (1, 0): [lambda: z_opposite(1)],
        (1, 2): [lambda: x_arrivals(3)],
        (1, 3): [lambda: x_arrivals(1)],
        (1, 6): [lambda: last_x(0)],
        (2, 1): [lambda: last_x(1)],
        (2, 4): [lambda: across_arrives(3), lambda: across_arrives(1)],
        (2, 6): [lambda: across_arrives(2)],
    }
    steps = 7

    def attend(g, step, only):
        for (group, at), acts in duties.items():
            if at in only:

                @pl.when(jnp.logical_and(g == group, step == at))
                def _(acts=acts):
                    for act in acts:
                        act()

    def pick(index, values):
        out = values[-1]
        for n in range(len(values) - 2, -1, -1):
            out = jnp.where(index == n, values[n], out)
        return out

    order = [
        ((0, 0, 0), (0, 0, 1)),
        ((0, 3, 0), (0, 1, 0)),
        ((0, 3, 1), (0, 1, 1)),
        ((3, 0, 0), (1, 0, 0)),
        ((3, 0, 1), (1, 0, 1)),
        ((0, 2, 0), (0, 2, 1)),
        ((3, 3, 0), (3, 1, 0)),
        ((1, 3, 0), (1, 1, 0)),
        ((3, 3, 1), (3, 1, 1)),
        ((1, 3, 1), (1, 1, 1)),
        ((2, 0, 0), (2, 0, 1)),
        ((2, 3, 0), (2, 1, 0)),
        ((2, 3, 1), (2, 1, 1)),
        ((3, 2, 0), (1, 2, 0)),
        ((3, 2, 1), (1, 2, 1)),
        ((2, 2, 0), (2, 2, 1)),
    ]
    for n, pair in enumerate(order):
        for m, spot in enumerate(pair):
            when[2 * n + m] = times[ident(*spot)]

    @pl.loop(0, EPOCHS // GROUP)
    def _(g):
        @pl.loop(0, 4)
        def _(j):
            attend(g, j, range(4))
            step = 4 * g + j
            blocks = []
            for m in range(2):
                dz, dx, other = [pick(step, [pair[m][axis] for pair in order]) for axis in range(3)]
                blocks.append(ident(dz, dx, other))

                @pl.when(other == 1)
                def _():
                    arrived(blocks[m])

            for m, block in enumerate(blocks):
                move_rows(
                    block, when[2 * step + m], 2 * j + m, ty, vel, hyps, images, row_tmpl, rhs.at[m], moved
                )

        @pl.loop(0, hyps // 2)
        def _(pair):
            attend(g, pair + 4, range(4, steps))
            for n in range(2):
                add_columns(2 * pair + n, g * GROUP, when, vel, col_main, col_rim, moved, acc)

    for n, (block, part, peer) in enumerate(sends):
        descriptor(block, part, peer, n).wait_send()

    @pl.loop(0, hyps)
    def _(h):
        sums = acc[h]
        out[h] = (sums[:, :ROWS] / jnp.sqrt(sums[:, ROWS:])).T


def shards(science, inv_variance, psf_taps, epoch_times, velocities):
    hyps = velocities.shape[0]
    vmem = pl.BlockSpec(memory_space=pltpu.VMEM)
    smem = pl.BlockSpec(memory_space=pltpu.SMEM)
    depth = GROUP * SPAN
    return pl.pallas_call(
        functools.partial(kernel, hyps),
        out_shape=jax.ShapeDtypeStruct((hyps, ROWS, COLS), F32),
        in_specs=[smem, smem, smem, vmem, vmem, vmem],
        out_specs=vmem,
        scratch_shapes=[
            pltpu.VMEM((EPOCHS, 3, SPAN, 128), BF16),
            pltpu.VMEM((2, ROWS + 2 * EDGE, COLS), F32),
            pltpu.VMEM((3, COLS + 2 * EDGE, 128), F32),
            pltpu.VMEM((FRACS, 2, 320, 128), F32),
            pltpu.VMEM((FRACS, 320, 128), F32),
            pltpu.VMEM((FRACS, 256, 128), F32),
            pltpu.VMEM((2, 256, hyps * ROWS), BF16),
            pltpu.VMEM((hyps, depth, 256), BF16),
            pltpu.VMEM((hyps, COLS, 256), F32),
            pltpu.SMEM((EPOCHS,), jnp.int32),
            pltpu.SemaphoreType.DMA((3,)),
            pltpu.SemaphoreType.DMA((3,)),
            pltpu.SemaphoreType.DMA((64,)),
            pltpu.SemaphoreType.DMA((EPOCHS, 2)),
        ],
        compiler_params=pltpu.CompilerParams(collective_id=0, has_side_effects=True, vmem_limit_bytes=56 << 20),
    )(epoch_times, velocities.T, jnp.asarray(spline_table()), psf_taps, science, inv_variance)


def solution(mesh):
    in_specs = (P("ea", "tx", "ty"), P("ea", "tx", "ty"), P("ea", None), P(), P("ea", None))
    out_specs = P("ea", "tx", "ty")
    return jax.shard_map(shards, mesh=mesh, in_specs=in_specs, out_specs=out_specs, check_vma=False)
```
